256 devices in a mesh: band: 4 (over z_lo, core), slab: 64 (over y, x, z_hi).
Axes of the slice: x: 4, y: 4, z: 8 (z_hi: 4, z_lo: 2; z = z_hi * 2 + z_lo), core: 2. Of those that a mesh axis runs over, the one named last changes fastest.
Arguments:
- orbitals: float32 [16, 128, 128, 128], P('band', 'slab'), may hold values from -6 to 6
Outputs:
- spectrum: float32 [128, 128, 128], P('slab', None, 'band')
The draws below stay inside these ranges and needn't reach their ends.
All inputs are finite; a program needn't handle non-finite values.
Results may differ from the reference program's by a relative error of at most 0.0043.
Values may be sent and summed in bfloat16 or wider, within the bound.
A program may use at most 64 MiB of HBM per device.

```python
import math
import jax
import jax.numpy as jnp
from jax import lax

NG = 128
ORB_DEV = 4
SHIFTS = 2
ORBITALS = 16
N_BAND = 4


def steps_of(key, extent, split, least, largest):
    def one(position, parts):
        steps = jax.random.uniform(jax.random.fold_in(jax.random.fold_in(key, 6), position), (parts,), jnp.float32, least / len(split), largest / len(split))
        return jnp.repeat(jnp.exp(steps), extent[position] // parts).reshape((-1,) + (1,) * (len(extent) - position - 1))

    loudness = one(*split[0])
    for cut in split[1:]:
        loudness = loudness * one(*cut)
    return loudness


def centred(stream_key, dims, width, most, pieces=(), kind=jnp.bfloat16):
    loudness = steps_of(stream_key, dims, pieces, -0.22, 0.18) if pieces else 1.0
    values = jax.random.normal(stream_key, dims, jnp.float32) * width * loudness
    return jnp.minimum(jnp.maximum(values, -most), most).astype(kind)


def setup_inputs(seed: int = 0) -> dict:
    splits = jax.random.split(jax.random.key(seed), 2)
    orbitals = centred(splits[0], (ORBITALS, NG, NG, NG), 1.0, 6.0, ((0, 4), (1, 64)), jnp.float32)
    return dict(orbitals=orbitals)


def dft_tables(grid_len):
    positions = jnp.arange(grid_len, dtype=jnp.int32)
    phase = positions[:, None] * positions[None, :] % grid_len
    angle = phase.astype(jnp.float32) * (2.0 * math.pi / grid_len)
    factor = 1.0 / math.sqrt(grid_len)
    cosine = jnp.cos(angle) * factor
    sine = -jnp.sin(angle) * factor
    real_table = jnp.stack([cosine, sine]).astype(jnp.bfloat16)
    complex_table = jnp.stack([jnp.stack([cosine, -sine]), jnp.stack([sine, cosine])]).astype(jnp.bfloat16)
    return (real_table, complex_table)

def transform_pairs(pairs, real_table, complex_table):
    first_pass = jnp.einsum('pxyz,dkz->pdxyk', pairs.astype(jnp.float32), real_table).astype(jnp.bfloat16)
    second_pass = jnp.einsum('pcxyz,dcky->pdxkz', first_pass.astype(jnp.float32), complex_table).astype(jnp.bfloat16)
    third_pass = jnp.einsum('pcxyz,dckx->pdkyz', second_pass.astype(jnp.float32), complex_table)
    return lax.optimization_barrier(jnp.sum(third_pass * third_pass, axis=(0, 1)))

def reference(orbitals):
    real_table, complex_table = dft_tables(NG)
    real_wide = real_table.astype(jnp.float32)
    complex_wide = complex_table.astype(jnp.float32)
    blocks = orbitals.reshape(N_BAND, ORB_DEV, NG, NG, NG)

    def accumulate(running, flat_index):
        band_block = flat_index // (SHIFTS * ORB_DEV)
        remainder = flat_index % (SHIFTS * ORB_DEV)
        shift_amount = remainder // ORB_DEV + 1
        row_index = remainder % ORB_DEV
        own_block = lax.dynamic_index_in_dim(blocks, band_block, 0, keepdims=False)
        own_row = lax.dynamic_index_in_dim(own_block, row_index, 0, keepdims=True)
        partner_index = ((band_block - shift_amount) % N_BAND).astype(jnp.int32)
        partner = lax.dynamic_index_in_dim(blocks, partner_index, 0, keepdims=False)
        pairs = (own_row * partner).astype(jnp.bfloat16)
        return (running + transform_pairs(pairs, real_wide, complex_wide), None)
    start = jnp.zeros((NG, NG, NG), jnp.float32)
    indices = jnp.arange(N_BAND * SHIFTS * ORB_DEV, dtype=jnp.int32)
    accumulated, _ = lax.scan(accumulate, start, indices)
    pair_count = float(N_BAND * SHIFTS * ORB_DEV * ORB_DEV)
    return accumulated / pair_count
```

```python
import functools
import math

import jax
import jax.numpy as jnp
import ml_dtypes
import numpy as np
from jax import lax
from jax.experimental import pallas as pl
from jax.experimental.pallas import tpu as pltpu
from jax.sharding import PartitionSpec as P

MESH = pl.DeviceIdType.MESH
NG = 128
BF16 = ml_dtypes.bfloat16
EDGES = ((0, 1, 1.0), (1, 2, 1.0), (0, 2, 2.0))


def ky_order():
    rows = [0, 64, 1, 127]
    for d in range(1, 32):
        rows += [2 * d, 128 - 2 * d, 2 * d + 1, 127 - 2 * d]
    return np.array(rows)


def kx_order():
    return np.array([8 * yx + 2 * zh + e for zh in range(4) for e in range(2) for yx in range(16)])


def tables():
    n = np.arange(NG)
    angle = ((n[:, None] * n[None]) % NG).astype(np.float32) * np.float32(2.0 * math.pi / NG)
    factor = np.float32(1.0 / math.sqrt(NG))
    c = (np.cos(angle) * factor).astype(BF16).astype(np.float32)
    s = (-np.sin(angle) * factor).astype(BF16).astype(np.float32)
    ky, kx = ky_order(), kx_order()
    first = np.block([[c.T, s.T], [-s.T, c.T]])
    second = np.block([[c[ky], -s[ky]], [s[ky], c[ky]]])
    third = np.zeros((2, 2, NG, 32, 2, 2, 4), np.float32)
    src, x4 = np.arange(32)[:, None], np.arange(4)[None]
    x_global = (src // 2) * 8 + x4 * 2 + src % 2
    cx, sx = c[kx][:, x_global], s[kx][:, x_global]
    for q in range(2):
        third[q, 0, :, :, q, 0] = cx
        third[q, 0, :, :, q, 1] = -sx
        third[q, 1, :, :, q, 0] = sx
        third[q, 1, :, :, q, 1] = cx
    third = third.reshape(512, 512)
    mirror = ((kx[:, None] + kx[None]) % NG == 0).astype(np.float32)
    spread = np.zeros((2, 4, NG, 4, 4, 32), np.float32)
    partner = (1, 0, 3, 2)
    for slot in range(4):
        for b in range(4):
            for k in range(32):
                kz = 32 * b + k
                spread[0, slot, kz, b, slot, k] = 1
                spread[1, partner[slot], -kz % NG, b, slot, k] = 1
    spread = spread.reshape(1024, 512)
    place = np.zeros((2, 4, NG, NG), np.float32)
    for e in range(2):
        for slot in range(4):
            for d in range(32):
                place[e, slot, ky[d * 4 + slot], (d // 2) * 8 + (d % 2) * 2 + e] = 1
    place = place.reshape(1024, NG)
    return [t.astype(BF16) for t in (first, second, third, mirror, spread, place)]


def dot(a, b):
    return jnp.dot(a, b, preferred_element_type=jnp.float32)


def kernel(
    x_hbm, t1_hbm, t2_hbm, t3_hbm, mir_hbm, spr_hbm, plc_hbm, out_ref,
    x_ref, t1, t2, t3, mir, spr, plc,
    own, orb, prod, first_out, grid_rows, msg, got, power, u_ref, r1, v_ref, s2, r2,
    load_sem, g_send, g_recv, a_send, a_recv, u_send, u_recv, s_send, s_recv,
):
    band, slab = lax.axis_index("band"), lax.axis_index("slab")
    zl, c = lax.div(band, 2), lax.rem(band, 2)
    y, x, zh = lax.div(slab, 16), lax.rem(lax.div(slab, 4), 4), lax.rem(slab, 4)
    z = 2 * zh + zl
    yx = y * 4 + x
    d_me = yx * 2 + c

    def line(z_to, c_to):
        return {"band": lax.rem(z_to, 2) * 2 + c_to, "slab": yx * 4 + lax.div(z_to, 2)}

    def plane(yx_to, c_to):
        return {"band": zl * 2 + c_to, "slab": yx_to * 4 + zh}

    barrier = pltpu.get_barrier_semaphore()

    def greet(to):
        pl.semaphore_signal(barrier, inc=1, device_id=to, device_id_type=MESH)

    def greet_line(i, _):
        greet(line(lax.rem(z + lax.div(i, 2), 8), lax.rem(c + i, 2)))
        return 0

    def plane_peer(i):
        dyx, dc = lax.div(i, 2), lax.rem(i, 2)
        y_to = lax.rem(y + lax.div(dyx, 4), 4)
        x_to = lax.rem(x + lax.rem(dyx, 4), 4)
        return y_to * 4 + x_to, lax.rem(c + dc, 2)

    def greet_plane(i, _):
        greet(plane(*plane_peer(i)))
        return 0

    lax.fori_loop(1, 16, greet_line, 0)
    lax.fori_loop(2, 32, greet_plane, 0)
    loads = []
    for i, (a, b) in enumerate(
        ((x_hbm, x_ref), (t1_hbm, t1), (t2_hbm, t2), (t3_hbm, t3), (mir_hbm, mir), (spr_hbm, spr), (plc_hbm, plc))
    ):
        loads.append(pltpu.make_async_copy(a, b, load_sem.at[i]))
        loads[-1].start()
    loads[0].wait()
    for e in range(2):
        own[e] = x_ref[:, e].astype(jnp.bfloat16)
    v_ref[...] = jnp.zeros_like(v_ref)
    pl.semaphore_wait(barrier, 45)

    def gather_parts(j, p, c_to):
        m = lax.rem(band + 3 - j, 4)
        twist = (1 - lax.rem(m, 2)) * c + lax.rem(m + lax.div(m, 2), 2) * zl
        h = lax.rem(p + twist, 2)
        z_to = 2 * (2 * p + lax.rem(m, 2)) + 1 - lax.div(m, 2)
        src = own.at[c_to, pl.ds(2 * h, 2)]
        dst = orb.at[j, zh]
        here = jnp.logical_and(z_to == z, c_to == c)
        i = j * 4 + p * 2 + c_to

        def local_copy():
            return pltpu.make_async_copy(src, dst, g_recv.at[j, zh])

        def far_copy():
            return pltpu.make_async_remote_copy(
                src, dst, g_send.at[i], g_recv.at[j, zh], device_id=line(z_to, c_to), device_id_type=MESH
            )

        return here, local_copy, far_copy

    for j in range(3):
        for p in range(2):
            for c_to in range(2):
                here, local_copy, far_copy = gather_parts(j, p, c_to)
                pl.when(here)(lambda: local_copy().start())
                pl.when(jnp.logical_not(here))(lambda: far_copy().start())

    def wait_slot(j):
        for k in range(4):
            pltpu.make_async_copy(orb.at[j, k], orb.at[j, k], g_recv.at[j, k]).wait()

    def exchange(g, i):
        yx_to, c_to = plane_peer(i)
        d_to = yx_to * 2 + c_to
        return pltpu.make_async_remote_copy(
            msg.at[g, d_to], got.at[g, :, pl.ds(pl.multiple_of(d_me * 16, 16), 16)],
            a_send.at[g, i], a_recv.at[g], device_id=plane(yx_to, c_to), device_id_type=MESH,
        )

    loads[1].wait()
    loads[2].wait()
    for g, (ja, jb, _) in enumerate(EDGES):
        if g == 0:
            wait_slot(0)
            wait_slot(1)
        elif g == 1:
            wait_slot(2)

        def one_q(q, _):
            for k in range(4):
                left = orb[ja, k, q]
                for part in range(2):
                    prod[pl.ds(k * NG, NG), pl.ds(part * NG, NG)] = left * orb[jb, k, part]
            first_out[...] = dot(prod[...], t1[...]).astype(jnp.bfloat16)
            for k in range(4):
                rows = first_out[pl.ds(k * NG, NG), :]
                stacked = jnp.concatenate([rows[:, :NG], rows[:, NG:]], axis=0)
                second = dot(t2[...], stacked)
                grid_rows[q, pl.ds(k * NG, NG), :] = second[:NG]
                grid_rows[q, pl.ds((4 + k) * NG, NG), :] = second[NG:]
            return 0

        lax.fori_loop(0, 2, one_q, 0)

        def turn(d, _):
            for slot in range(4):
                halves = [grid_rows[q, pl.ds(d * 4 + slot, 8, stride=NG), :] for q in range(2)]
                msg[g, d, slot] = jnp.concatenate(halves, axis=0).astype(jnp.bfloat16)
            return 0

        lax.fori_loop(0, 32, turn, 0)

        def send(i, _):
            exchange(g, i).start()
            return 0

        lax.fori_loop(1, 32, send, 0)
        pltpu.make_async_copy(
            msg.at[g, d_me], got.at[g, :, pl.ds(pl.multiple_of(d_me * 16, 16), 16)], a_recv.at[g]
        ).start()

    loads[3].wait()
    for g, (_, _, weight) in enumerate(EDGES):
        pltpu.make_async_copy(got.at[g], got.at[g], a_recv.at[g]).wait()

        def one_ky(slot, _):
            f = dot(t3[...], got[g, slot])
            total = f[:128] * f[:128] + f[128:256] * f[128:256] + f[256:384] * f[256:384] + f[384:] * f[384:]
            if g == 0:
                power[slot] = total
            else:
                power[slot] += total * weight
            return 0

        lax.fori_loop(0, 4, one_ky, 0)

    loads[4].wait()
    loads[5].wait()
    direct = jnp.concatenate([power[i] for i in range(4)], axis=1).astype(jnp.bfloat16)
    flipped = dot(mir[...], direct).astype(jnp.bfloat16)
    f0, f1 = flipped[:, :128], flipped[:, 128:256]
    alone = d_me == 0
    flipped = jnp.concatenate([jnp.where(alone, f1, f0), jnp.where(alone, f0, f1), flipped[:, 256:]], axis=1)
    both = (dot(direct, spr[:512]) + dot(flipped, spr[512:])) * (1.0 / 256.0)
    for a in range(4):
        for b in range(4):
            u_ref[a, b] = both[a * 32 : a * 32 + 32, b * 128 : b * 128 + 128].astype(jnp.bfloat16)

    def reduce_copy(i):
        z_to, c_to = lax.rem(z + lax.div(i, 2), 8), lax.rem(c + i, 2)
        return pltpu.make_async_remote_copy(
            u_ref.at[lax.div(z_to, 2), lax.rem(z_to, 2) * 2 + c_to], r1.at[z * 2 + c],
            u_send.at[i], u_recv, device_id=line(z_to, c_to), device_id_type=MESH,
        )

    def reduce_send(i, _):
        reduce_copy(i).start()
        return 0

    lax.fori_loop(1, 16, reduce_send, 0)
    pltpu.make_async_copy(u_ref.at[zh, band], r1.at[z * 2 + c], u_recv).start()
    pltpu.make_async_copy(r1, r1, u_recv).wait()
    for cs in range(2):
        total = r1[cs].astype(jnp.float32)
        for k in range(1, 8):
            total += r1[2 * k + cs].astype(jnp.float32)
        v_ref[pl.ds(cs * 32, 32), :] = total
    for k in range(16):
        s2[k] = v_ref[pl.ds(k, 8, stride=16), :]

    def owner_copy(i):
        yx_to, c_to = plane_peer(2 * i)
        return pltpu.make_async_remote_copy(
            s2.at[yx_to], r2.at[yx], s_send.at[i], s_recv, device_id=plane(yx_to, c_to), device_id_type=MESH
        )

    def owner_send(i, _):
        owner_copy(i).start()
        return 0

    lax.fori_loop(1, 16, owner_send, 0)
    pltpu.make_async_copy(s2.at[yx], r2.at[yx], s_recv).start()
    loads[6].wait()
    pltpu.make_async_copy(r2, r2, s_recv).wait()
    rows = r2[...].reshape(128, 128)
    high = rows.astype(jnp.bfloat16)
    low = (rows - high.astype(jnp.float32)).astype(jnp.bfloat16)
    placed = dot(plc[...], high) + dot(plc[...], low)
    for e in range(2):
        total = None
        for slot in range(4):
            part = placed[(e * 4 + slot) * 128 : (e * 4 + slot + 1) * 128, slot * 32 : slot * 32 + 32]
            total = part if total is None else total + part
        out_ref[e] = total

    for j in range(3):
        for p in range(2):
            for c_to in range(2):
                here, _, far_copy = gather_parts(j, p, c_to)
                pl.when(jnp.logical_not(here))(lambda: far_copy().wait_send())
    for g in range(3):

        def sent(i, _):
            exchange(g, i).wait_send()
            return 0

        lax.fori_loop(1, 32, sent, 0)

    def sent_small(i, _):
        reduce_copy(i).wait_send()
        owner_copy(i).wait_send()
        return 0

    lax.fori_loop(1, 16, sent_small, 0)


def solution(mesh):
    consts = tables()
    vm, bf, f32 = pltpu.VMEM, jnp.bfloat16, jnp.float32

    def local(orbitals):
        return pl.pallas_call(
            kernel,
            out_shape=jax.ShapeDtypeStruct((2, NG, 32), f32),
            in_specs=[pl.BlockSpec(memory_space=pl.ANY)] * 7,
            out_specs=pl.BlockSpec(memory_space=pltpu.VMEM),
            scratch_shapes=[
                vm((4, 2, NG, NG), f32),
                vm((256, 256), bf), vm((256, 256), bf), vm((512, 512), bf),
                vm((128, 128), bf), vm((1024, 512), bf), vm((1024, 128), bf),
                vm((2, 4, NG, NG), bf),
                vm((3, 4, 2, NG, NG), bf),
                vm((512, 256), bf),
                vm((512, 256), bf),
                vm((2, 1024, 128), f32),
                vm((3, 32, 4, 16, 128), bf),
                vm((3, 4, 512, 128), bf),
                vm((4, 128, 128), f32),
                vm((4, 4, 32, 128), bf),
                vm((16, 32, 128), bf),
                vm((128, 128), f32),
                vm((16, 8, 128), f32),
                vm((16, 8, 128), f32),
                pltpu.SemaphoreType.DMA((7,)),
                pltpu.SemaphoreType.DMA((12,)),
                pltpu.SemaphoreType.DMA((3, 4)),
                pltpu.SemaphoreType.DMA((3, 32)),
                pltpu.SemaphoreType.DMA((3,)),
                pltpu.SemaphoreType.DMA((16,)),
                pltpu.SemaphoreType.DMA,
                pltpu.SemaphoreType.DMA((16,)),
                pltpu.SemaphoreType.DMA,
            ],
            compiler_params=pltpu.CompilerParams(collective_id=0, has_side_effects=True),
        )(orbitals, *[jnp.asarray(t) for t in consts])

    return jax.shard_map(
        local,
        mesh=mesh,
        in_specs=(P("band", "slab", None, None),),
        out_specs=P("slab", None, "band"),
        check_vma=False,
    )
```

```python
import functools
import math

import jax
import jax.numpy as jnp
import ml_dtypes
import numpy as np
from jax import lax
from jax.experimental import pallas as pl
from jax.experimental.pallas import tpu as pltpu
from jax.sharding import PartitionSpec as P

MESH = pl.DeviceIdType.MESH
NG = 128
BF16 = ml_dtypes.bfloat16
PIECES = ((0, 0), (1, 0), (1, 1), (0, 1), (2, 0), (2, 1))
UNITS = ((3, 0, 0, 1, 1.0), (4, 0, 1, 1, 1.0), (5, 2, 0, 1, 1.0), (5, 2, 0, 0, 2.0), (6, 2, 1, 1, 1.0), (6, 2, 1, 0, 2.0))


def ky_order():
    rows = [0, 64, 1, 127]
    for d in range(1, 32):
        rows += [2 * d, 128 - 2 * d, 2 * d + 1, 127 - 2 * d]
    return np.array(rows)


def kx_order():
    return np.array([8 * yx + 2 * zh + e for zh in range(4) for e in range(2) for yx in range(16)])


def tables():
    n = np.arange(NG)
    angle = ((n[:, None] * n[None]) % NG).astype(np.float32) * np.float32(2.0 * math.pi / NG)
    factor = np.float32(1.0 / math.sqrt(NG))
    c = (np.cos(angle) * factor).astype(BF16).astype(np.float32)
    s = (-np.sin(angle) * factor).astype(BF16).astype(np.float32)
    ky, kx = ky_order(), kx_order()
    first = np.block([[c.T, s.T], [-s.T, c.T]])
    second = np.block([[c[ky], -s[ky]], [s[ky], c[ky]]])
    third = np.zeros((2, 2, NG, 32, 2, 2, 4), np.float32)
    src, x4 = np.arange(32)[:, None], np.arange(4)[None]
    x_global = (src // 2) * 8 + x4 * 2 + src % 2
    cx, sx = c[kx][:, x_global], s[kx][:, x_global]
    for q in range(2):
        third[q, 0, :, :, q, 0] = cx
        third[q, 0, :, :, q, 1] = -sx
        third[q, 1, :, :, q, 0] = sx
        third[q, 1, :, :, q, 1] = cx
    third = third.reshape(512, 512)
    mirror = ((kx[:, None] + kx[None]) % NG == 0).astype(np.float32)
    spread = np.zeros((2, 4, NG, 4, 4, 32), np.float32)
    partner = (1, 0, 3, 2)
    for slot in range(4):
        for b in range(4):
            for k in range(32):
                kz = 32 * b + k
                spread[0, slot, kz, b, slot, k] = 1
                spread[1, partner[slot], -kz % NG, b, slot, k] = 1
    spread = spread.reshape(1024, 512)
    place = np.zeros((2, 4, NG, NG), np.float32)
    for e in range(2):
        for slot in range(4):
            for d in range(32):
                place[e, slot, ky[d * 4 + slot], (d // 2) * 8 + (d % 2) * 2 + e] = 1
    place = place.reshape(1024, NG)
    return [t.astype(BF16) for t in (first, second, third, mirror, spread, place)]


def dot(a, b):
    return jnp.dot(a, b, preferred_element_type=jnp.float32)


def kernel(
    x_hbm, t1_hbm, t2_hbm, t3_hbm, mir_hbm, spr_hbm, plc_hbm, out_ref,
    x_ref, t1, t2, t3, mir, spr, plc,
    own, orb, prod, first_out, grid_rows, msg, got, power, u_ref, r1, v_ref, s2, r2,
    load_sem, g_send, g_recv, a_send, a_recv, u_send, u_recv, s_send, s_recv,
):
    band, slab = lax.axis_index("band"), lax.axis_index("slab")
    zl, c = lax.div(band, 2), lax.rem(band, 2)
    y, x, zh = lax.div(slab, 16), lax.rem(lax.div(slab, 4), 4), lax.rem(slab, 4)
    z = 2 * zh + zl
    yx = y * 4 + x
    d_me = yx * 2 + c

    def line(z_to, c_to):
        return {"band": lax.rem(z_to, 2) * 2 + c_to, "slab": yx * 4 + lax.div(z_to, 2)}

    def plane(yx_to, c_to):
        return {"band": zl * 2 + c_to, "slab": yx_to * 4 + zh}

    barrier = pltpu.get_barrier_semaphore()

    def greet(to):
        pl.semaphore_signal(barrier, inc=1, device_id=to, device_id_type=MESH)

    def greet_line(i, _):
        greet(line(lax.rem(z + lax.div(i, 2), 8), lax.rem(c + i, 2)))
        return 0

    def plane_peer(i):
        dyx, dc = lax.div(i, 2), lax.rem(i, 2)
        y_to = lax.rem(y + lax.div(dyx, 4), 4)
        x_to = lax.rem(x + lax.rem(dyx, 4), 4)
        return y_to * 4 + x_to, lax.rem(c + dc, 2)

    def greet_plane(i, _):
        greet(plane(*plane_peer(i)))
        return 0

    lax.fori_loop(1, 16, greet_line, 0)
    lax.fori_loop(2, 32, greet_plane, 0)
    loads = []
    for i, (a, b) in enumerate(
        ((x_hbm, x_ref), (t1_hbm, t1), (t2_hbm, t2), (t3_hbm, t3), (mir_hbm, mir), (spr_hbm, spr), (plc_hbm, plc))
    ):
        loads.append(pltpu.make_async_copy(a, b, load_sem.at[i]))
        loads[-1].start()
    loads[0].wait()
    for e in range(2):
        own[e] = x_ref[:, e].astype(jnp.bfloat16)
    v_ref[...] = jnp.zeros_like(v_ref)
    pl.semaphore_wait(barrier, 45)

    def gather_parts(n, p, c_to):
        j, o = PIECES[n]
        m = lax.rem(band + 3 - j, 4)
        twist = (1 - lax.rem(m, 2)) * c + lax.rem(m + lax.div(m, 2), 2) * zl
        h = lax.rem(p + twist, 2)
        z_to = 2 * (2 * p + lax.rem(m, 2)) + 1 - lax.div(m, 2)
        src = own.at[c_to, 2 * h + o]
        dst = orb.at[j, zh, o]
        here = jnp.logical_and(z_to == z, c_to == c)

        def local_copy():
            return pltpu.make_async_copy(src, dst, g_recv.at[n, zh])

        def far_copy():
            return pltpu.make_async_remote_copy(
                src, dst, g_send.at[n, p * 2 + c_to], g_recv.at[n, zh], device_id=line(z_to, c_to), device_id_type=MESH
            )

        return here, local_copy, far_copy

    for n in range(6):
        for p in range(2):
            for c_to in range(2):
                here, local_copy, far_copy = gather_parts(n, p, c_to)
                pl.when(here)(lambda: local_copy().start())
                pl.when(jnp.logical_not(here))(lambda: far_copy().start())

    def wait_piece(n):
        j, o = PIECES[n]
        for k in range(4):
            pltpu.make_async_copy(orb.at[j, k, o], orb.at[j, k, o], g_recv.at[n, k]).wait()

    def exchange(g, i):
        yx_to, c_to = plane_peer(i)
        d_to = yx_to * 2 + c_to
        return pltpu.make_async_remote_copy(
            msg.at[g, d_to], got.at[g, :, pl.ds(pl.multiple_of(d_me * 16, 16), 16)],
            a_send.at[g], a_recv.at[g], device_id=plane(yx_to, c_to), device_id_type=MESH,
        )

    loads[1].wait()
    loads[2].wait()
    held = 0
    for g, (needs, jl, ol, jr, _) in enumerate(UNITS):
        while held < needs:
            wait_piece(held)
            held += 1
        for k in range(4):
            left = orb[jl, k, ol]
            for part in range(2):
                prod[pl.ds(k * NG, NG), pl.ds(part * NG, NG)] = left * orb[jr, k, part]
        first_out[...] = dot(prod[...], t1[...]).astype(jnp.bfloat16)
        for k in range(4):
            rows = first_out[pl.ds(k * NG, NG), :]
            stacked = jnp.concatenate([rows[:, :NG], rows[:, NG:]], axis=0)
            second = dot(t2[...], stacked)
            grid_rows[pl.ds(k * NG, NG), :] = second[:NG]
            grid_rows[pl.ds((4 + k) * NG, NG), :] = second[NG:]

        def turn(d, _):
            for pair in range(2):
                both_ky = [grid_rows[pl.ds(d * 4 + pair * 2 + i, 8, stride=NG), :] for i in range(2)]
                msg[g, d, pair] = jnp.concatenate(both_ky, axis=0).astype(jnp.bfloat16)
            return 0

        lax.fori_loop(0, 32, turn, 0, unroll=4)

        def send(i, _):
            exchange(g, i).start()
            return 0

        lax.fori_loop(1, 32, send, 0)
        pltpu.make_async_copy(
            msg.at[g, d_me], got.at[g, :, pl.ds(pl.multiple_of(d_me * 16, 16), 16)], a_recv.at[g]
        ).start()

    loads[3].wait()
    for g, (_, _, _, _, weight) in enumerate(UNITS):
        pltpu.make_async_copy(got.at[g], got.at[g], a_recv.at[g]).wait()
        for pair in range(2):
            f = dot(t3[...], got[g, pair])
            for i in range(2):
                re, im = f[i * 256 : i * 256 + 128], f[i * 256 + 128 : i * 256 + 256]
                total = re * re + im * im
                if g == 0:
                    power[pair * 2 + i] = total
                else:
                    power[pair * 2 + i] += total * weight

    loads[4].wait()
    loads[5].wait()
    direct = jnp.concatenate([power[i] for i in range(4)], axis=1).astype(jnp.bfloat16)
    flipped = dot(mir[...], direct).astype(jnp.bfloat16)
    f0, f1 = flipped[:, :128], flipped[:, 128:256]
    alone = d_me == 0
    flipped = jnp.concatenate([jnp.where(alone, f1, f0), jnp.where(alone, f0, f1), flipped[:, 256:]], axis=1)
    both = (dot(direct, spr[:512]) + dot(flipped, spr[512:])) * (1.0 / 256.0)
    for a in range(4):
        for b in range(4):
            u_ref[a, b] = both[a * 32 : a * 32 + 32, b * 128 : b * 128 + 128].astype(jnp.bfloat16)

    def reduce_copy(i):
        z_to, c_to = lax.rem(z + lax.div(i, 2), 8), lax.rem(c + i, 2)
        return pltpu.make_async_remote_copy(
            u_ref.at[lax.div(z_to, 2), lax.rem(z_to, 2) * 2 + c_to], r1.at[z * 2 + c],
            u_send, u_recv, device_id=line(z_to, c_to), device_id_type=MESH,
        )

    def reduce_send(i, _):
        reduce_copy(i).start()
        return 0

    lax.fori_loop(1, 16, reduce_send, 0)
    pltpu.make_async_copy(u_ref.at[zh, band], r1.at[z * 2 + c], u_recv).start()
    for n in range(6):
        for p in range(2):
            for c_to in range(2):
                here, _, far_copy = gather_parts(n, p, c_to)
                pl.when(jnp.logical_not(here))(lambda: far_copy().wait_send())
    for g in range(6):
        pltpu.make_async_copy(msg.at[g, pl.ds(0, 31)], msg.at[g, pl.ds(0, 31)], a_send.at[g]).wait()
    pltpu.make_async_copy(r1.at[pl.ds(0, 15)], r1.at[pl.ds(0, 15)], u_send).wait()
    pltpu.make_async_copy(r1, r1, u_recv).wait()
    for cs in range(2):
        total = r1[cs].astype(jnp.float32)
        for k in range(1, 8):
            total += r1[2 * k + cs].astype(jnp.float32)
        v_ref[pl.ds(cs * 32, 32), :] = total
    for k in range(16):
        s2[k] = v_ref[pl.ds(k, 8, stride=16), :]

    def owner_copy(i):
        yx_to, c_to = plane_peer(2 * i)
        return pltpu.make_async_remote_copy(
            s2.at[yx_to], r2.at[yx], s_send, s_recv, device_id=plane(yx_to, c_to), device_id_type=MESH
        )

    def owner_send(i, _):
        owner_copy(i).start()
        return 0

    lax.fori_loop(1, 16, owner_send, 0)
    pltpu.make_async_copy(s2.at[yx], r2.at[yx], s_recv).start()
    loads[6].wait()
    pltpu.make_async_copy(r2, r2, s_recv).wait()
    rows = r2[...].reshape(128, 128)
    high = rows.astype(jnp.bfloat16)
    low = (rows - high.astype(jnp.float32)).astype(jnp.bfloat16)
    placed = dot(plc[...], high) + dot(plc[...], low)
    for e in range(2):
        total = None
        for slot in range(4):
            part = placed[(e * 4 + slot) * 128 : (e * 4 + slot + 1) * 128, slot * 32 : slot * 32 + 32]
            total = part if total is None else total + part
        out_ref[e] = total

    pltpu.make_async_copy(r2.at[pl.ds(0, 15)], r2.at[pl.ds(0, 15)], s_send).wait()


def solution(mesh):
    consts = tables()
    vm, bf, f32 = pltpu.VMEM, jnp.bfloat16, jnp.float32

    def local(orbitals):
        return pl.pallas_call(
            kernel,
            out_shape=jax.ShapeDtypeStruct((2, NG, 32), f32),
            in_specs=[pl.BlockSpec(memory_space=pl.ANY)] * 7,
            out_specs=pl.BlockSpec(memory_space=pltpu.VMEM),
            scratch_shapes=[
                vm((4, 2, NG, NG), f32),
                vm((256, 256), bf), vm((256, 256), bf), vm((512, 512), bf),
                vm((128, 128), bf), vm((1024, 512), bf), vm((1024, 128), bf),
                vm((2, 4, NG, NG), bf),
                vm((3, 4, 2, NG, NG), bf),
                vm((512, 256), bf),
                vm((512, 256), bf),
                vm((1024, 128), f32),
                vm((6, 32, 2, 16, 128), bf),
                vm((6, 2, 512, 128), bf),
                vm((4, 128, 128), f32),
                vm((4, 4, 32, 128), bf),
                vm((16, 32, 128), bf),
                vm((128, 128), f32),
                vm((16, 8, 128), f32),
                vm((16, 8, 128), f32),
                pltpu.SemaphoreType.DMA((7,)),
                pltpu.SemaphoreType.DMA((6, 4)),
                pltpu.SemaphoreType.DMA((6, 4)),
                pltpu.SemaphoreType.DMA((6,)),
                pltpu.SemaphoreType.DMA((6,)),
                pltpu.SemaphoreType.DMA,
                pltpu.SemaphoreType.DMA,
                pltpu.SemaphoreType.DMA,
                pltpu.SemaphoreType.DMA,
            ],
            compiler_params=pltpu.CompilerParams(collective_id=0, has_side_effects=True),
        )(orbitals, *[jnp.asarray(t) for t in consts])

    return jax.shard_map(
        local,
        mesh=mesh,
        in_specs=(P("band", "slab", None, None),),
        out_specs=P("slab", None, "band"),
        check_vma=False,
    )
```

```python
import functools
import math

import jax
import jax.numpy as jnp
import ml_dtypes
import numpy as np
from jax import lax
from jax.experimental import pallas as pl
from jax.experimental.pallas import tpu as pltpu
from jax.sharding import PartitionSpec as P

MESH = pl.DeviceIdType.MESH
NG = 128
BF16 = ml_dtypes.bfloat16
PIECES = ((0, 0), (1, 0), (1, 1), (0, 1), (2, 0), (2, 1))
UNITS = ((3, 0, 0, 1, 1.0), (4, 0, 1, 1, 1.0), (5, 2, 0, 1, 1.0), (5, 2, 0, 0, 2.0), (6, 2, 1, 1, 1.0), (6, 2, 1, 0, 2.0))


AHEAD = 3


def ky_order():
    rows = [0, 64, 1, 127]
    for d in range(1, 32):
        rows += [2 * d, 128 - 2 * d, 2 * d + 1, 127 - 2 * d]
    return np.array(rows)


def kx_order():
    return np.array([8 * yx + 2 * zh + e for zh in range(4) for e in range(2) for yx in range(16)])


def tables():
    n = np.arange(NG)
    angle = ((n[:, None] * n[None]) % NG).astype(np.float32) * np.float32(2.0 * math.pi / NG)
    factor = np.float32(1.0 / math.sqrt(NG))
    c = (np.cos(angle) * factor).astype(BF16).astype(np.float32)
    s = (-np.sin(angle) * factor).astype(BF16).astype(np.float32)
    ky, kx = ky_order(), kx_order()
    first = np.block([[c.T, s.T], [-s.T, c.T]])
    second = np.block([[c[ky], -s[ky]], [s[ky], c[ky]]])
    third = np.zeros((2, 2, NG, 32, 2, 2, 4), np.float32)
    src, x4 = np.arange(32)[:, None], np.arange(4)[None]
    x_global = (src // 2) * 8 + x4 * 2 + src % 2
    cx, sx = c[kx][:, x_global], s[kx][:, x_global]
    for q in range(2):
        third[q, 0, :, :, q, 0] = cx
        third[q, 0, :, :, q, 1] = -sx
        third[q, 1, :, :, q, 0] = sx
        third[q, 1, :, :, q, 1] = cx
    third = third.reshape(512, 512)
    mirror = ((kx[:, None] + kx[None]) % NG == 0).astype(np.float32)
    spread = np.zeros((2, 4, NG, 4, 4, 32), np.float32)
    partner = (1, 0, 3, 2)
    for slot in range(4):
        for b in range(4):
            for k in range(32):
                kz = 32 * b + k
                spread[0, slot, kz, b, slot, k] = 1
                spread[1, partner[slot], -kz % NG, b, slot, k] = 1
    spread = spread.reshape(1024, 512)
    place = np.zeros((2, 4, NG, NG), np.float32)
    for e in range(2):
        for slot in range(4):
            for d in range(32):
                place[e, slot, ky[d * 4 + slot], (d // 2) * 8 + (d % 2) * 2 + e] = 1
    place = place.reshape(1024, NG)
    return [t.astype(BF16) for t in (first, second, third, mirror, spread, place)]


def dot(a, b):
    return jnp.dot(a, b, preferred_element_type=jnp.float32)


def kernel(
    x_hbm, t1_hbm, t2_hbm, t3_hbm, mir_hbm, spr_hbm, plc_hbm, out_ref,
    x_ref, t1, t2, t3, mir, spr, plc,
    own, orb, prod, first_out, grid_rows, msg, got, power, u_ref, r1, v_ref, s2, r2,
    load_sem, g_send, g_recv, a_send, a_recv, u_send, u_recv, s_send, s_recv,
):
    band, slab = lax.axis_index("band"), lax.axis_index("slab")
    zl, c = lax.div(band, 2), lax.rem(band, 2)
    y, x, zh = lax.div(slab, 16), lax.rem(lax.div(slab, 4), 4), lax.rem(slab, 4)
    z = 2 * zh + zl
    yx = y * 4 + x
    d_me = yx * 2 + c

    def line(z_to, c_to):
        return {"band": lax.rem(z_to, 2) * 2 + c_to, "slab": yx * 4 + lax.div(z_to, 2)}

    def plane(yx_to, c_to):
        return {"band": zl * 2 + c_to, "slab": yx_to * 4 + zh}

    barrier = pltpu.get_barrier_semaphore()

    def greet(to):
        pl.semaphore_signal(barrier, inc=1, device_id=to, device_id_type=MESH)

    def greet_line(i, _):
        greet(line(lax.rem(z + lax.div(i, 2), 8), lax.rem(c + i, 2)))
        return 0

    def plane_peer(i):
        dyx, dc = lax.div(i, 2), lax.rem(i, 2)
        y_to = lax.rem(y + lax.div(dyx, 4), 4)
        x_to = lax.rem(x + lax.rem(dyx, 4), 4)
        return y_to * 4 + x_to, lax.rem(c + dc, 2)

    def greet_plane(i, _):
        greet(plane(*plane_peer(i)))
        return 0

    lax.fori_loop(1, 16, greet_line, 0)
    lax.fori_loop(2, 32, greet_plane, 0)
    loads = []
    for i, (a, b) in enumerate(
        ((x_hbm, x_ref), (t1_hbm, t1), (t2_hbm, t2), (t3_hbm, t3), (mir_hbm, mir), (spr_hbm, spr), (plc_hbm, plc))
    ):
        loads.append(pltpu.make_async_copy(a, b, load_sem.at[i]))
        loads[-1].start()
    loads[0].wait()
    for e in range(2):
        own[e] = x_ref[:, e].astype(jnp.bfloat16)
    v_ref[...] = jnp.zeros_like(v_ref)
    pl.semaphore_wait(barrier, 45)

    def gather_parts(n, p, c_to):
        j, o = PIECES[n]
        m = lax.rem(band + 3 - j, 4)
        twist = (1 - lax.rem(m, 2)) * c + lax.rem(m + lax.div(m, 2), 2) * zl
        h = lax.rem(p + twist, 2)
        z_to = 2 * (2 * p + lax.rem(m, 2)) + 1 - lax.div(m, 2)
        src = own.at[c_to, 2 * h + o]
        dst = orb.at[j, zh, o]
        here = jnp.logical_and(z_to == z, c_to == c)

        def local_copy():
            return pltpu.make_async_copy(src, dst, g_recv.at[n, zh])

        def far_copy():
            return pltpu.make_async_remote_copy(
                src, dst, g_send.at[n, p * 2 + c_to], g_recv.at[n, zh], device_id=line(z_to, c_to), device_id_type=MESH
            )

        return here, local_copy, far_copy

    def start_piece(n):
        for p in range(2):
            for c_to in range(2):
                here, local_copy, far_copy = gather_parts(n, p, c_to)
                pl.when(here)(lambda: local_copy().start())
                pl.when(jnp.logical_not(here))(lambda: far_copy().start())

    for n in range(AHEAD):
        start_piece(n)

    def wait_piece(n):
        j, o = PIECES[n]
        for k in range(4):
            pltpu.make_async_copy(orb.at[j, k, o], orb.at[j, k, o], g_recv.at[n, k]).wait()

    def exchange(g, i):
        yx_to, c_to = plane_peer(i)
        d_to = yx_to * 2 + c_to
        return pltpu.make_async_remote_copy(
            msg.at[g, d_to], got.at[g, :, pl.ds(pl.multiple_of(d_me * 16, 16), 16)],
            a_send.at[g], a_recv.at[g], device_id=plane(yx_to, c_to), device_id_type=MESH,
        )

    loads[1].wait()
    loads[2].wait()
    held = 0
    for g, (needs, jl, ol, jr, _) in enumerate(UNITS):
        while held < needs:
            wait_piece(held)
            if held + AHEAD < 6:
                start_piece(held + AHEAD)
            held += 1
        for k in range(4):
            left = orb[jl, k, ol]
            for part in range(2):
                prod[pl.ds(k * NG, NG), pl.ds(part * NG, NG)] = left * orb[jr, k, part]
        first_out[...] = dot(prod[...], t1[...]).astype(jnp.bfloat16)
        for k in range(4):
            rows = first_out[pl.ds(k * NG, NG), :]
            stacked = jnp.concatenate([rows[:, :NG], rows[:, NG:]], axis=0)
            second = dot(t2[...], stacked)
            grid_rows[pl.ds(k * NG, NG), :] = second[:NG]
            grid_rows[pl.ds((4 + k) * NG, NG), :] = second[NG:]

        def turn(d, _):
            for pair in range(2):
                both_ky = [grid_rows[pl.ds(d * 4 + pair * 2 + i, 8, stride=NG), :] for i in range(2)]
                msg[g, d, pair] = jnp.concatenate(both_ky, axis=0).astype(jnp.bfloat16)
            return 0

        lax.fori_loop(0, 32, turn, 0, unroll=4)

        def send(i, _):
            exchange(g, i).start()
            return 0

        lax.fori_loop(1, 32, send, 0)
        pltpu.make_async_copy(
            msg.at[g, d_me], got.at[g, :, pl.ds(pl.multiple_of(d_me * 16, 16), 16)], a_recv.at[g]
        ).start()

    loads[3].wait()
    for g, (_, _, _, _, weight) in enumerate(UNITS):
        pltpu.make_async_copy(got.at[g], got.at[g], a_recv.at[g]).wait()
        for pair in range(2):
            f = dot(t3[...], got[g, pair])
            for i in range(2):
                re, im = f[i * 256 : i * 256 + 128], f[i * 256 + 128 : i * 256 + 256]
                total = re * re + im * im
                if g == 0:
                    power[pair * 2 + i] = total
                else:
                    power[pair * 2 + i] += total * weight

    loads[4].wait()
    loads[5].wait()
    direct = jnp.concatenate([power[i] for i in range(4)], axis=1).astype(jnp.bfloat16)
    flipped = dot(mir[...], direct).astype(jnp.bfloat16)
    f0, f1 = flipped[:, :128], flipped[:, 128:256]
    alone = d_me == 0
    flipped = jnp.concatenate([jnp.where(alone, f1, f0), jnp.where(alone, f0, f1), flipped[:, 256:]], axis=1)
    both = (dot(direct, spr[:512]) + dot(flipped, spr[512:])) * (1.0 / 256.0)
    for a in range(4):
        for b in range(4):
            u_ref[a, b] = both[a * 32 : a * 32 + 32, b * 128 : b * 128 + 128].astype(jnp.bfloat16)

    def reduce_copy(i):
        z_to, c_to = lax.rem(z + lax.div(i, 2), 8), lax.rem(c + i, 2)
        return pltpu.make_async_remote_copy(
            u_ref.at[lax.div(z_to, 2), lax.rem(z_to, 2) * 2 + c_to], r1.at[z * 2 + c],
            u_send, u_recv, device_id=line(z_to, c_to), device_id_type=MESH,
        )

    def reduce_send(i, _):
        reduce_copy(i).start()
        return 0

    lax.fori_loop(1, 16, reduce_send, 0)
    pltpu.make_async_copy(u_ref.at[zh, band], r1.at[z * 2 + c], u_recv).start()
    for n in range(6):
        for p in range(2):
            for c_to in range(2):
                here, _, far_copy = gather_parts(n, p, c_to)
                pl.when(jnp.logical_not(here))(lambda: far_copy().wait_send())
    for g in range(6):
        pltpu.make_async_copy(msg.at[g, pl.ds(0, 31)], msg.at[g, pl.ds(0, 31)], a_send.at[g]).wait()
    pltpu.make_async_copy(r1.at[pl.ds(0, 15)], r1.at[pl.ds(0, 15)], u_send).wait()
    pltpu.make_async_copy(r1, r1, u_recv).wait()
    for cs in range(2):
        total = r1[cs].astype(jnp.float32)
        for k in range(1, 8):
            total += r1[2 * k + cs].astype(jnp.float32)
        v_ref[pl.ds(cs * 32, 32), :] = total
    for k in range(16):
        s2[k] = v_ref[pl.ds(k, 8, stride=16), :]

    def owner_copy(i):
        yx_to, c_to = plane_peer(2 * i)
        return pltpu.make_async_remote_copy(
            s2.at[yx_to], r2.at[yx], s_send, s_recv, device_id=plane(yx_to, c_to), device_id_type=MESH
        )

    def owner_send(i, _):
        owner_copy(i).start()
        return 0

    lax.fori_loop(1, 16, owner_send, 0)
    pltpu.make_async_copy(s2.at[yx], r2.at[yx], s_recv).start()
    loads[6].wait()
    pltpu.make_async_copy(r2, r2, s_recv).wait()
    rows = r2[...].reshape(128, 128)
    high = rows.astype(jnp.bfloat16)
    low = (rows - high.astype(jnp.float32)).astype(jnp.bfloat16)
    placed = dot(plc[...], high) + dot(plc[...], low)
    for e in range(2):
        total = None
        for slot in range(4):
            part = placed[(e * 4 + slot) * 128 : (e * 4 + slot + 1) * 128, slot * 32 : slot * 32 + 32]
            total = part if total is None else total + part
        out_ref[e] = total

    pltpu.make_async_copy(r2.at[pl.ds(0, 15)], r2.at[pl.ds(0, 15)], s_send).wait()


def solution(mesh):
    consts = tables()
    vm, bf, f32 = pltpu.VMEM, jnp.bfloat16, jnp.float32

    def local(orbitals):
        return pl.pallas_call(
            kernel,
            out_shape=jax.ShapeDtypeStruct((2, NG, 32), f32),
            in_specs=[pl.BlockSpec(memory_space=pl.ANY)] * 7,
            out_specs=pl.BlockSpec(memory_space=pltpu.VMEM),
            scratch_shapes=[
                vm((4, 2, NG, NG), f32),
                vm((256, 256), bf), vm((256, 256), bf), vm((512, 512), bf),
                vm((128, 128), bf), vm((1024, 512), bf), vm((1024, 128), bf),
                vm((2, 4, NG, NG), bf),
                vm((3, 4, 2, NG, NG), bf),
                vm((512, 256), bf),
                vm((512, 256), bf),
                vm((1024, 128), f32),
                vm((6, 32, 2, 16, 128), bf),
                vm((6, 2, 512, 128), bf),
                vm((4, 128, 128), f32),
                vm((4, 4, 32, 128), bf),
                vm((16, 32, 128), bf),
                vm((128, 128), f32),
                vm((16, 8, 128), f32),
                vm((16, 8, 128), f32),
                pltpu.SemaphoreType.DMA((7,)),
                pltpu.SemaphoreType.DMA((6, 4)),
                pltpu.SemaphoreType.DMA((6, 4)),
                pltpu.SemaphoreType.DMA((6,)),
                pltpu.SemaphoreType.DMA((6,)),
                pltpu.SemaphoreType.DMA,
                pltpu.SemaphoreType.DMA,
                pltpu.SemaphoreType.DMA,
                pltpu.SemaphoreType.DMA,
            ],
            compiler_params=pltpu.CompilerParams(collective_id=0, has_side_effects=True),
        )(orbitals, *[jnp.asarray(t) for t in consts])

    return jax.shard_map(
        local,
        mesh=mesh,
        in_specs=(P("band", "slab", None, None),),
        out_specs=P("slab", None, "band"),
        check_vma=False,
    )
```

```python
import functools
import math

import jax
import jax.numpy as jnp
import ml_dtypes
import numpy as np
from jax import lax
from jax.experimental import pallas as pl
from jax.experimental.pallas import tpu as pltpu
from jax.sharding import PartitionSpec as P

MESH = pl.DeviceIdType.MESH
NG = 128
BF16 = ml_dtypes.bfloat16
PIECES = ((0, 0), (1, 0), (1, 1), (0, 1), (2, 0), (2, 1))
UNITS = ((3, 0, 0, 1, 1.0), (4, 0, 1, 1, 1.0), (5, 2, 0, 1, 1.0), (5, 2, 0, 0, 2.0), (6, 2, 1, 1, 1.0), (6, 2, 1, 0, 2.0))


AHEAD = 3


def ky_order():
    rows = [0, 64, 1, 127]
    for d in range(1, 32):
        rows += [2 * d, 128 - 2 * d, 2 * d + 1, 127 - 2 * d]
    return np.array(rows)


def kx_order():
    return np.array([8 * yx + 2 * zh + e for zh in range(4) for e in range(2) for yx in range(16)])


def tables():
    n = np.arange(NG)
    angle = ((n[:, None] * n[None]) % NG).astype(np.float32) * np.float32(2.0 * math.pi / NG)
    factor = np.float32(1.0 / math.sqrt(NG))
    c = (np.cos(angle) * factor).astype(BF16).astype(np.float32)
    s = (-np.sin(angle) * factor).astype(BF16).astype(np.float32)
    ky, kx = ky_order(), kx_order()
    first = np.block([[c.T, s.T], [-s.T, c.T]])
    second = np.block([[c[ky], -s[ky]], [s[ky], c[ky]]])
    third = np.zeros((2, 2, NG, 32, 2, 2, 4), np.float32)
    src, x4 = np.arange(32)[:, None], np.arange(4)[None]
    x_global = (src // 2) * 8 + x4 * 2 + src % 2
    cx, sx = c[kx][:, x_global], s[kx][:, x_global]
    for q in range(2):
        third[q, 0, :, :, q, 0] = cx
        third[q, 0, :, :, q, 1] = -sx
        third[q, 1, :, :, q, 0] = sx
        third[q, 1, :, :, q, 1] = cx
    third = third.reshape(512, 512)
    mirror = ((kx[:, None] + kx[None]) % NG == 0).astype(np.float32)
    spread = np.zeros((2, 4, NG, 4, 4, 32), np.float32)
    partner = (1, 0, 3, 2)
    for slot in range(4):
        for b in range(4):
            for k in range(32):
                kz = 32 * b + k
                spread[0, slot, kz, b, slot, k] = 1
                spread[1, partner[slot], -kz % NG, b, slot, k] = 1
    spread = spread.reshape(1024, 512)
    place = np.zeros((2, 4, NG, NG), np.float32)
    for e in range(2):
        for slot in range(4):
            for d in range(32):
                place[e, slot, ky[d * 4 + slot], (d // 2) * 8 + (d % 2) * 2 + e] = 1
    place = place.reshape(1024, NG)
    return [t.astype(BF16) for t in (first, second, third, mirror, spread, place)]


def dot(a, b):
    return jnp.dot(a, b, preferred_element_type=jnp.float32)


def kernel(
    x_hbm, t1_hbm, t2_hbm, t3_hbm, mir_hbm, spr_hbm, plc_hbm, out_ref,
    x_ref, t1, t2, t3, mir, spr, plc,
    own, orb, prod, first_out, grid_rows, msg, got, power, u_ref, r1, v_ref, s2, r2,
    load_sem, g_send, g_recv, a_send, a_recv, u_send, u_recv, s_send, s_recv,
):
    band, slab = lax.axis_index("band"), lax.axis_index("slab")
    zl, c = lax.div(band, 2), lax.rem(band, 2)
    y, x, zh = lax.div(slab, 16), lax.rem(lax.div(slab, 4), 4), lax.rem(slab, 4)
    z = 2 * zh + zl
    yx = y * 4 + x
    d_me = yx * 2 + c

    def line(z_to, c_to):
        return {"band": lax.rem(z_to, 2) * 2 + c_to, "slab": yx * 4 + lax.div(z_to, 2)}

    def plane(yx_to, c_to):
        return {"band": zl * 2 + c_to, "slab": yx_to * 4 + zh}

    barrier = pltpu.get_barrier_semaphore()

    def greet(to):
        pl.semaphore_signal(barrier, inc=1, device_id=to, device_id_type=MESH)

    def greet_line(i, _):
        greet(line(lax.rem(z + lax.div(i, 2), 8), lax.rem(c + i, 2)))
        return 0

    def plane_peer(i):
        dyx, dc = lax.div(i, 2), lax.rem(i, 2)
        y_to = lax.rem(y + lax.div(dyx, 4), 4)
        x_to = lax.rem(x + lax.rem(dyx, 4), 4)
        return y_to * 4 + x_to, lax.rem(c + dc, 2)

    def greet_plane(i, _):
        greet(plane(*plane_peer(i)))
        return 0

    lax.fori_loop(1, 16, greet_line, 0)
    lax.fori_loop(2, 32, greet_plane, 0)
    loads = []
    for i, (a, b) in enumerate(
        ((x_hbm, x_ref), (t1_hbm, t1), (t2_hbm, t2), (t3_hbm, t3), (mir_hbm, mir), (spr_hbm, spr), (plc_hbm, plc))
    ):
        loads.append(pltpu.make_async_copy(a, b, load_sem.at[i]))
        loads[-1].start()
    loads[0].wait()
    for e in range(2):
        own[e] = x_ref[:, e].astype(jnp.bfloat16)
    v_ref[...] = jnp.zeros_like(v_ref)
    pl.semaphore_wait(barrier, 45)

    def gather_parts(n, p, c_to):
        j, o = PIECES[n]
        m = lax.rem(band + 3 - j, 4)
        twist = (1 - lax.rem(m, 2)) * c + lax.rem(m + lax.div(m, 2), 2) * zl
        h = lax.rem(p + twist, 2)
        z_to = 2 * (2 * p + lax.rem(m, 2)) + 1 - lax.div(m, 2)
        src = own.at[c_to, 2 * h + o]
        dst = orb.at[j, zh, o]
        here = jnp.logical_and(z_to == z, c_to == c)

        def local_copy():
            return pltpu.make_async_copy(src, dst, g_recv.at[n, zh])

        def far_copy():
            return pltpu.make_async_remote_copy(
                src, dst, g_send.at[n, p * 2 + c_to], g_recv.at[n, zh], device_id=line(z_to, c_to), device_id_type=MESH
            )

        return here, local_copy, far_copy

    def start_piece(n):
        for p in range(2):
            for c_to in range(2):
                here, local_copy, far_copy = gather_parts(n, p, c_to)
                pl.when(here)(lambda: local_copy().start())
                pl.when(jnp.logical_not(here))(lambda: far_copy().start())

    for n in range(AHEAD):
        start_piece(n)

    def wait_piece(n):
        j, o = PIECES[n]
        for k in range(4):
            pltpu.make_async_copy(orb.at[j, k, o], orb.at[j, k, o], g_recv.at[n, k]).wait()

    def exchange(g, i):
        yx_to, c_to = plane_peer(i)
        d_to = yx_to * 2 + c_to
        return pltpu.make_async_remote_copy(
            msg.at[g, d_to], got.at[g, :, pl.ds(pl.multiple_of(d_me * 16, 16), 16)],
            a_send.at[g], a_recv.at[g], device_id=plane(yx_to, c_to), device_id_type=MESH,
        )

    loads[1].wait()
    loads[2].wait()
    held = 0
    for g, (needs, jl, ol, jr, _) in enumerate(UNITS):
        while held < needs:
            wait_piece(held)
            if held + AHEAD < 6:
                start_piece(held + AHEAD)
            held += 1
        for k in range(4):
            left = orb[jl, k, ol]
            for part in range(2):
                prod[pl.ds(k * NG, NG), pl.ds(part * NG, NG)] = left * orb[jr, k, part]
        first_out[...] = dot(prod[...], t1[...]).astype(jnp.bfloat16)
        for k in range(4):
            rows = first_out[pl.ds(k * NG, NG), :]
            stacked = jnp.concatenate([rows[:, :NG], rows[:, NG:]], axis=0)
            second = dot(t2[...], stacked)
            grid_rows[pl.ds(k * NG, NG), :] = second[:NG]
            grid_rows[pl.ds((4 + k) * NG, NG), :] = second[NG:]

        def turn(i):
            yx_to, c_to = plane_peer(i)
            d = yx_to * 2 + c_to
            for pair in range(2):
                both_ky = [grid_rows[pl.ds(d * 4 + pair * 2 + i, 8, stride=NG), :] for i in range(2)]
                msg[g, d, pair] = jnp.concatenate(both_ky, axis=0).astype(jnp.bfloat16)

        def send(i, _):
            turn(lax.rem(i + 1, 32))
            exchange(g, i).start()
            return 0

        turn(1)
        lax.fori_loop(1, 32, send, 0)
        pltpu.make_async_copy(
            msg.at[g, d_me], got.at[g, :, pl.ds(pl.multiple_of(d_me * 16, 16), 16)], a_recv.at[g]
        ).start()

    loads[3].wait()
    for g, (_, _, _, _, weight) in enumerate(UNITS):
        pltpu.make_async_copy(got.at[g], got.at[g], a_recv.at[g]).wait()
        for pair in range(2):
            f = dot(t3[...], got[g, pair])
            for i in range(2):
                re, im = f[i * 256 : i * 256 + 128], f[i * 256 + 128 : i * 256 + 256]
                total = re * re + im * im
                if g == 0:
                    power[pair * 2 + i] = total
                else:
                    power[pair * 2 + i] += total * weight

    loads[4].wait()
    loads[5].wait()
    direct = jnp.concatenate([power[i] for i in range(4)], axis=1).astype(jnp.bfloat16)
    flipped = dot(mir[...], direct).astype(jnp.bfloat16)
    f0, f1 = flipped[:, :128], flipped[:, 128:256]
    alone = d_me == 0
    flipped = jnp.concatenate([jnp.where(alone, f1, f0), jnp.where(alone, f0, f1), flipped[:, 256:]], axis=1)
    both = (dot(direct, spr[:512]) + dot(flipped, spr[512:])) * (1.0 / 256.0)
    for a in range(4):
        for b in range(4):
            u_ref[a, b] = both[a * 32 : a * 32 + 32, b * 128 : b * 128 + 128].astype(jnp.bfloat16)

    def reduce_copy(i):
        z_to, c_to = lax.rem(z + lax.div(i, 2), 8), lax.rem(c + i, 2)
        return pltpu.make_async_remote_copy(
            u_ref.at[lax.div(z_to, 2), lax.rem(z_to, 2) * 2 + c_to], r1.at[z * 2 + c],
            u_send, u_recv, device_id=line(z_to, c_to), device_id_type=MESH,
        )

    def reduce_send(i, _):
        reduce_copy(i).start()
        return 0

    lax.fori_loop(1, 16, reduce_send, 0)
    pltpu.make_async_copy(u_ref.at[zh, band], r1.at[z * 2 + c], u_recv).start()
    for n in range(6):
        for p in range(2):
            for c_to in range(2):
                here, _, far_copy = gather_parts(n, p, c_to)
                pl.when(jnp.logical_not(here))(lambda: far_copy().wait_send())
    for g in range(6):
        pltpu.make_async_copy(msg.at[g, pl.ds(0, 31)], msg.at[g, pl.ds(0, 31)], a_send.at[g]).wait()
    pltpu.make_async_copy(r1.at[pl.ds(0, 15)], r1.at[pl.ds(0, 15)], u_send).wait()
    pltpu.make_async_copy(r1, r1, u_recv).wait()
    for cs in range(2):
        total = r1[cs].astype(jnp.float32)
        for k in range(1, 8):
            total += r1[2 * k + cs].astype(jnp.float32)
        v_ref[pl.ds(cs * 32, 32), :] = total
    for k in range(16):
        s2[k] = v_ref[pl.ds(k, 8, stride=16), :]

    def owner_copy(i):
        yx_to, c_to = plane_peer(2 * i)
        return pltpu.make_async_remote_copy(
            s2.at[yx_to], r2.at[yx], s_send, s_recv, device_id=plane(yx_to, c_to), device_id_type=MESH
        )

    def owner_send(i, _):
        owner_copy(i).start()
        return 0

    lax.fori_loop(1, 16, owner_send, 0)
    pltpu.make_async_copy(s2.at[yx], r2.at[yx], s_recv).start()
    loads[6].wait()
    pltpu.make_async_copy(r2, r2, s_recv).wait()
    rows = r2[...].reshape(128, 128)
    high = rows.astype(jnp.bfloat16)
    low = (rows - high.astype(jnp.float32)).astype(jnp.bfloat16)
    placed = dot(plc[...], high) + dot(plc[...], low)
    for e in range(2):
        total = None
        for slot in range(4):
            part = placed[(e * 4 + slot) * 128 : (e * 4 + slot + 1) * 128, slot * 32 : slot * 32 + 32]
            total = part if total is None else total + part
        out_ref[e] = total

    pltpu.make_async_copy(r2.at[pl.ds(0, 15)], r2.at[pl.ds(0, 15)], s_send).wait()


def solution(mesh):
    consts = tables()
    vm, bf, f32 = pltpu.VMEM, jnp.bfloat16, jnp.float32

    def local(orbitals):
        return pl.pallas_call(
            kernel,
            out_shape=jax.ShapeDtypeStruct((2, NG, 32), f32),
            in_specs=[pl.BlockSpec(memory_space=pl.ANY)] * 7,
            out_specs=pl.BlockSpec(memory_space=pltpu.VMEM),
            scratch_shapes=[
                vm((4, 2, NG, NG), f32),
                vm((256, 256), bf), vm((256, 256), bf), vm((512, 512), bf),
                vm((128, 128), bf), vm((1024, 512), bf), vm((1024, 128), bf),
                vm((2, 4, NG, NG), bf),
                vm((3, 4, 2, NG, NG), bf),
                vm((512, 256), bf),
                vm((512, 256), bf),
                vm((1024, 128), f32),
                vm((6, 32, 2, 16, 128), bf),
                vm((6, 2, 512, 128), bf),
                vm((4, 128, 128), f32),
                vm((4, 4, 32, 128), bf),
                vm((16, 32, 128), bf),
                vm((128, 128), f32),
                vm((16, 8, 128), f32),
                vm((16, 8, 128), f32),
                pltpu.SemaphoreType.DMA((7,)),
                pltpu.SemaphoreType.DMA((6, 4)),
                pltpu.SemaphoreType.DMA((6, 4)),
                pltpu.SemaphoreType.DMA((6,)),
                pltpu.SemaphoreType.DMA((6,)),
                pltpu.SemaphoreType.DMA,
                pltpu.SemaphoreType.DMA,
                pltpu.SemaphoreType.DMA,
                pltpu.SemaphoreType.DMA,
            ],
            compiler_params=pltpu.CompilerParams(collective_id=0, has_side_effects=True),
        )(orbitals, *[jnp.asarray(t) for t in consts])

    return jax.shard_map(
        local,
        mesh=mesh,
        in_specs=(P("band", "slab", None, None),),
        out_specs=P("slab", None, "band"),
        check_vma=False,
    )
```
